32 devices in a mesh: dom: 4 (over x, core), blk: 8 (over z, y).
Axes of the slice: x: 2, y: 2, z: 4, core: 2. Of those that a mesh axis runs over, the one named last changes fastest.
Arguments:
- ginv: float32 [4, 2048, 2048], P('dom', 'blk'), as said below
- couple: float32 [4, 2048, 2048], P('dom', 'blk'), may hold values from -0.109375 to 0.109375
- arrow_rhs: float32 [4, 64, 2048], P('dom', None, 'blk'), may hold values from -6 to 6
- arrow_in: float32 [64, 2048], P(None, 'blk'), may hold values from -6 to 6
- tip_cov: float32 [64, 64], replicated, as said below
- bnd_next: float32 [64, 2048], P(None, 'blk'), may hold values from -6 to 6
Outputs:
- arrow_rows: float32 [4, 64, 2048], P('dom', None, 'blk')
- cross_cov: float32 [4, 64, 2048], P('dom', None, 'blk')
The draws below stay inside these ranges and needn't reach their ends.
Inputs may be any that keep to these rules, and one draw needn't show every extreme that they name: `ginv`: every block is zero above its diagonal, with diagonal entries between 0.5 and 1.5. `tip_cov`: Symmetric.
All inputs are finite; a program needn't handle non-finite values.
Results may differ from the reference program's by a relative error of at most 0.00013.
Values sent between devices are 32-bit elements; how exact they have to be, the bound alone decides.
A program may use at most 64 MiB of HBM per device.

```python
import jax
import jax.numpy as jnp
from jax import lax

B = 2048
A = 64
TSTEPS = 4


def draw_ginv(key, part):
    first_key, second_key = jax.random.split(jax.random.fold_in(key, 11))
    diagonal = jax.random.uniform(first_key, (TSTEPS, B), jnp.float32, 0.6, 1.4)
    lower_part = jax.random.normal(second_key, (TSTEPS, B, B), jnp.float32) * (0.6 / jnp.sqrt(B * 1.0))
    lower_part = jnp.tril(lower_part, -1)
    return lower_part + diagonal[:, :, None] * jnp.eye(B, dtype=jnp.float32)[None]


def draw_tip_cov(key, part):
    first_key, second_key = jax.random.split(jax.random.fold_in(key, 23))
    entries = jax.random.normal(first_key, (A, A), jnp.float32) * (0.3 / jnp.sqrt(A * 1.0))
    diagonal = jax.random.uniform(second_key, (A,), jnp.float32, 0.2, 0.6)
    return 0.5 * (entries + entries.T) + jnp.diag(diagonal)


def shard_levels(key, extent, cuts, smallest, top_value):
    factor_of = 1.0
    for dim, shards_of in cuts:
        heights = jax.random.uniform(jax.random.fold_in(jax.random.fold_in(key, 6), dim), (shards_of,), jnp.float32, smallest / len(cuts), top_value / len(cuts))
        factor_of = factor_of * jnp.repeat(jnp.exp(heights), extent[dim] // shards_of).reshape((-1,) + (1,) * (len(extent) - 1 - dim))
    return factor_of


def noise(own_key, shape, deviation, most, shards=(), kind=jnp.bfloat16):
    factor_of = shard_levels(own_key, shape, shards, -0.22, 0.18) if shards else 1.0
    values = jax.random.normal(own_key, shape, jnp.float32) * deviation * factor_of
    return jnp.minimum(jnp.maximum(values, -most), most).astype(kind)


def setup_inputs(seed: int = 0) -> dict:
    keys = jax.random.split(jax.random.key(seed), 7)
    return {
        "ginv": draw_ginv(jax.random.fold_in(keys[6], 71), 0),
        "couple": noise(keys[1], (TSTEPS, B, B), (B * 3 // 2) ** -0.5, 0.109375, ((0, 4), (1, 8)), jnp.float32),
        "arrow_rhs": noise(keys[2], (TSTEPS, A, B), 1.0, 6.0, ((0, 4), (2, 8)), jnp.float32),
        "arrow_in": noise(keys[3], (A, B), 1.0, 6.0, ((1, 8),), jnp.float32),
        "tip_cov": draw_tip_cov(jax.random.fold_in(keys[6], 71), 0),
        "bnd_next": noise(keys[5], (A, B), 1.0, 6.0, ((1, 8),), jnp.float32),
    }


highest = lax.Precision.HIGHEST


def reference(ginv, couple, arrow_rhs, arrow_in, tip_cov, bnd_next):
    step_count = ginv.shape[0]
    row_list = []
    previous = arrow_in
    for step_index in range(step_count):
        update = arrow_rhs[step_index] - jnp.dot(previous, couple[step_index].T, precision=highest)
        arrow_row = jnp.dot(update, ginv[step_index].T, precision=highest)
        row_list.append(arrow_row)
        previous = arrow_row
    onward = bnd_next
    cov_list = [None] * step_count
    for step_index in range(step_count - 1, -1, -1):
        combined = onward + jnp.dot(tip_cov, row_list[step_index], precision=highest)
        covariance = -jnp.dot(combined, ginv[step_index], precision=highest)
        cov_list[step_index] = covariance
        onward = jnp.dot(covariance, couple[step_index], precision=highest)
    return jnp.stack(row_list), jnp.stack(cov_list)
```

```python
import functools

import jax
import jax.numpy as jnp
from jax import lax
from jax.experimental import pallas as pl
from jax.experimental.pallas import tpu as pltpu
from jax.sharding import PartitionSpec as P

CHUNKS = 2
MESH = pl.DeviceIdType.MESH
NT = (((1,), (1,)), ((), ()))
NN = (((1,), (0,)), ((), ()))


def halves(x):
    head = x.astype(jnp.bfloat16)
    rest = (x - head.astype(jnp.float32)).astype(jnp.bfloat16)
    return head, rest


def stacked(x):
    head, rest = halves(x)
    return jnp.concatenate([head, rest], axis=0)


def product(pair, w_head, w_rest, dims):
    rows = pair.shape[0] // 2
    both = lax.dot_general(pair, w_head, dims, preferred_element_type=jnp.float32)
    cross = lax.dot_general(pair[:rows], w_rest, dims, preferred_element_type=jnp.float32)
    return both[:rows] + (both[rows:] + cross)


def around(n):
    order = []
    for k in range(1, n // 2 + 1):
        order += [k] if k == n - k else [k, n - k]
    return order


def kernel(
    turns, n, chunks,
    g_hbm, e_hbm, rhs_hbm, ain_hbm, tip_hbm, bnd_hbm,
    rows_out, cov_out,
    g_raw, e_raw, g_head, g_rest, e_head, e_rest, rhs, tip, bnd,
    prev_in, mid_in, cov_in, on_in, mid_mine, row_mine, cov_part, on_part,
    load_sem, send_sem, recv_sem,
):
    t = lax.axis_index("dom")
    me = lax.axis_index("blk")
    a, w = rhs.shape
    part = a // chunks
    near = around(n)
    far = near[::-1]

    loads = [
        pltpu.make_async_copy(src, dst, load_sem.at[i])
        for i, (src, dst) in enumerate(
            [(e_hbm.at[0], e_raw), (rhs_hbm.at[0], rhs), (g_hbm.at[0], g_raw), (tip_hbm, tip), (bnd_hbm, bnd)]
        )
    ]
    for load in loads:
        load.start()

    barrier = pltpu.get_barrier_semaphore()

    def greet(dom, blk):
        pl.semaphore_signal(barrier, inc=1, device_id=(dom, blk), device_id_type=MESH)

    for k in near:
        greet(t, lax.rem(me + k, n))

    @pl.when(t > 0)
    def _():
        for k in range(n):
            greet(t - 1, lax.rem(me + k, n))

    @pl.when(t < turns - 1)
    def _():
        for k in range(n):
            greet(t + 1, lax.rem(me + k, n))

    def rows_of(c):
        return pl.ds(c * part, part)

    def send(stage, c, slot, src, dst, dst_sem, dom, blk):
        return pltpu.make_async_remote_copy(
            src_ref=src, dst_ref=dst, send_sem=send_sem.at[stage, c, slot], recv_sem=dst_sem,
            device_id=(dom, blk), device_id_type=MESH,
        )

    def arrived(stage, c, j, ref):
        pltpu.make_async_copy(ref.at[c, j], ref.at[c, j], recv_sem.at[stage, c, j]).wait()

    def arrow_copies(c):
        return [
            send(0, c, k, ain_hbm.at[rows_of(c)], prev_in.at[c, me], recv_sem.at[0, c, me], t, lax.rem(me + k, n))
            for k in far
        ]

    def own_arrow(c):
        return pltpu.make_async_copy(ain_hbm.at[rows_of(c)], prev_in.at[c, me], recv_sem.at[0, c, me])

    def mid_copy(c, k):
        return send(1, c, k, mid_mine.at[c], mid_in.at[c, me], recv_sem.at[1, c, me], t, me + k)

    def row_copies(c):
        return [
            send(2, c, k, row_mine.at[rows_of(c)], prev_in.at[c, me], recv_sem.at[0, c, me], t + 1, lax.rem(me + k, n))
            for k in far + [0]
        ]

    def cov_copy(c, k):
        return send(3, c, k, cov_part.at[c, me - k], cov_in.at[c, me], recv_sem.at[2, c, me], t, me - k)

    def on_copy(c, k):
        blk = lax.rem(me + k, n)
        return send(4, c, k, on_part.at[c, blk], on_in.at[c, me], recv_sem.at[3, c, me], t - 1, blk)

    greeted = n - 1 + n * jnp.where(t > 0, 1, 0) + n * jnp.where(t < turns - 1, 1, 0)
    pl.semaphore_wait(barrier, greeted)

    @pl.when(t == 0)
    def _():
        for c in range(chunks):
            own_arrow(c).start()
            for copy in arrow_copies(c):
                copy.start()

    loads[0].wait()
    for j in range(n):
        e_head[j], e_rest[j] = halves(e_raw[:, j * w:(j + 1) * w])
    loads[1].wait()
    loads[2].wait()
    for j in range(n):
        g_head[j], g_rest[j] = halves(g_raw[:, j * w:(j + 1) * w])
    loads[3].wait()
    loads[4].wait()

    for c in range(chunks):
        total = rhs[rows_of(c), :]
        for k in [0] + near:
            j = lax.rem(me + k, n)
            arrived(0, c, j, prev_in)
            total = total - product(stacked(prev_in[c, j]), e_head[j], e_rest[j], NT)
        mid_mine[c] = total
        for k in range(n - 1, 0, -1):
            @pl.when(me + k < n)
            def _(c=c, k=k):
                mid_copy(c, k).start()

    for c in range(chunks):
        row_mine[rows_of(c), :] = product(stacked(mid_mine[c]), g_head[me], g_rest[me], NT)
        for k in range(1, n):
            @pl.when(me - k >= 0)
            def _(c=c, k=k):
                j = me - k
                arrived(1, c, j, mid_in)
                row_mine[rows_of(c), :] += product(stacked(mid_in[c, j]), g_head[j], g_rest[j], NT)

        @pl.when(t < turns - 1)
        def _(c=c):
            for copy in row_copies(c):
                copy.start()

    rows_out[0] = row_mine[...]
    tip_term = jnp.dot(tip[...], row_mine[...], precision=lax.Precision.HIGHEST)
    bnd[...] = jnp.where(t == turns - 1, bnd[...], 0.0) + tip_term

    for c in range(chunks):
        @pl.when(t < turns - 1)
        def _(c=c):
            for k in [0] + near:
                j = lax.rem(me + k, n)
                arrived(3, c, j, on_in)
                bnd[rows_of(c), :] += on_in[c, j]

        pair = stacked(-bnd[rows_of(c), :])
        for k in range(n - 1, 0, -1):
            @pl.when(me - k >= 0)
            def _(c=c, k=k, pair=pair):
                j = me - k
                cov_part[c, j] = product(pair, g_head[j], g_rest[j], NN)
                cov_copy(c, k).start()
        cov_out[0, rows_of(c), :] = product(pair, g_head[me], g_rest[me], NN)

    for c in range(chunks):
        for k in range(1, n):
            @pl.when(me + k < n)
            def _(c=c, k=k):
                arrived(2, c, me + k, cov_in)
                cov_out[0, rows_of(c), :] += cov_in[c, me + k]

        @pl.when(t > 0)
        def _(c=c):
            pair = stacked(cov_out[0, rows_of(c), :])
            for k in far + [0]:
                j = lax.rem(me + k, n)
                on_part[c, j] = product(pair, e_head[j], e_rest[j], NN)
                on_copy(c, k).start()

    for c in range(chunks):
        @pl.when(t == 0)
        def _(c=c):
            for copy in arrow_copies(c):
                copy.wait_send()

        @pl.when(t < turns - 1)
        def _(c=c):
            for copy in row_copies(c):
                copy.wait_send()

        for k in range(1, n):
            @pl.when(me + k < n)
            def _(c=c, k=k):
                mid_copy(c, k).wait_send()

            @pl.when(me - k >= 0)
            def _(c=c, k=k):
                cov_copy(c, k).wait_send()

        @pl.when(t > 0)
        def _(c=c):
            for k in range(n):
                on_copy(c, k).wait_send()


def solution(mesh):
    turns, n = mesh.shape["dom"], mesh.shape["blk"]

    def on_device(ginv, couple, arrow_rhs, arrow_in, tip_cov, bnd_next):
        a, w = arrow_in.shape
        whole = ginv.shape[2]
        chunks = CHUNKS
        part = a // chunks
        f32, bf16 = jnp.float32, jnp.bfloat16
        shape = jax.ShapeDtypeStruct((1, a, w), f32)
        blocks = pltpu.VMEM((chunks, n, part, w), f32)
        split = pltpu.VMEM((n, w, w), bf16)
        rows, cov = pl.pallas_call(
            functools.partial(kernel, turns, n, chunks),
            out_shape=(shape, shape),
            in_specs=[pl.BlockSpec(memory_space=pl.ANY)] * 6,
            out_specs=(pl.BlockSpec(memory_space=pltpu.VMEM),) * 2,
            scratch_shapes=[
                pltpu.VMEM((w, whole), f32),
                pltpu.VMEM((w, whole), f32),
                split, split, split, split,
                pltpu.VMEM((a, w), f32),
                pltpu.VMEM((a, a), f32),
                pltpu.VMEM((a, w), f32),
                blocks, blocks, blocks, blocks,
                pltpu.VMEM((chunks, part, w), f32),
                pltpu.VMEM((a, w), f32),
                blocks, blocks,
                pltpu.SemaphoreType.DMA((5,)),
                pltpu.SemaphoreType.DMA((5, chunks, n)),
                pltpu.SemaphoreType.DMA((4, chunks, n)),
            ],
            compiler_params=pltpu.CompilerParams(
                collective_id=0, has_side_effects=True, vmem_limit_bytes=48 * 1024 * 1024
            ),
        )(ginv, couple, arrow_rhs, arrow_in, tip_cov, bnd_next)
        return rows, cov

    return jax.shard_map(
        on_device,
        mesh=mesh,
        in_specs=(
            P("dom", "blk", None),
            P("dom", "blk", None),
            P("dom", None, "blk"),
            P(None, "blk"),
            P(),
            P(None, "blk"),
        ),
        out_specs=(P("dom", None, "blk"), P("dom", None, "blk")),
        check_vma=False,
    )
```

```python
import functools

import jax
import jax.numpy as jnp
from jax import lax
from jax.experimental import pallas as pl
from jax.experimental.pallas import tpu as pltpu
from jax.sharding import PartitionSpec as P

CHUNKS = 2


def ORDER(pairs):
    return range(1, pairs)


def PUT(routes, side):
    return [side] + routes

MESH = pl.DeviceIdType.MESH
NT = (((1,), (1,)), ((), ()))
NN = (((1,), (0,)), ((), ()))


def halves(x):
    head = x.astype(jnp.bfloat16)
    rest = (x - head.astype(jnp.float32)).astype(jnp.bfloat16)
    return head, rest


def stacked(x):
    head, rest = halves(x)
    return jnp.concatenate([head, rest], axis=0)


def product(pair, w_head, w_rest, dims):
    rows = pair.shape[0] // 2
    both = lax.dot_general(pair, w_head, dims, preferred_element_type=jnp.float32)
    cross = lax.dot_general(pair[:rows], w_rest, dims, preferred_element_type=jnp.float32)
    return both[:rows] + (both[rows:] + cross)


def around(n):
    order = []
    for k in range(1, n // 2 + 1):
        order += [k] if k == n - k else [k, n - k]
    return order


def kernel(
    turns, n, chunks,
    g_hbm, e_hbm, rhs_hbm, ain_hbm, tip_hbm, bnd_hbm,
    rows_out, cov_out,
    g_raw, e_raw, g_head, g_rest, e_head, e_rest, rhs, tip, bnd,
    prev_in, mid_in, cov_in, on_in, mid_mine, row_mine, cov_part, on_part,
    load_sem, send_sem, recv_sem,
):
    t = lax.axis_index("dom")
    me = lax.axis_index("blk")
    a, w = rhs.shape
    part = a // chunks
    near = around(n)
    pairs = n // 2
    p, y = lax.div(me, 2), lax.rem(me, 2)
    buddy = me + 1 - 2 * y
    before, after = t - 1, t + 1
    up, down, full = [], [], []
    for d in ORDER(pairs):
        for across in (1, 0):
            high = (p + d < pairs, 2 * (p + d) + (1 - y if across else y))
            low = (p - d >= 0, 2 * (p - d) + (1 - y if across else y))
            up.append(high)
            down.append(low)
            full += [high, low]
    side = (y >= 0, buddy)
    up, down, full = PUT(up, (y == 0, buddy)), PUT(down, (y == 1, buddy)), PUT(full, side)

    loads = [
        pltpu.make_async_copy(src, dst, load_sem.at[i])
        for i, (src, dst) in enumerate(
            [(e_hbm.at[0], e_raw), (rhs_hbm.at[0], rhs), (g_hbm.at[0], g_raw), (tip_hbm, tip), (bnd_hbm, bnd)]
        )
    ]
    for load in loads:
        load.start()

    barrier = pltpu.get_barrier_semaphore()

    def greet(dom, blk):
        pl.semaphore_signal(barrier, inc=1, device_id=(dom, blk), device_id_type=MESH)

    for k in near:
        greet(t, lax.rem(me + k, n))

    @pl.when(t > 0)
    def _():
        for k in range(n):
            greet(t - 1, lax.rem(me + k, n))

    @pl.when(t < turns - 1)
    def _():
        for k in range(n):
            greet(t + 1, lax.rem(me + k, n))

    def rows_of(c):
        return pl.ds(c * part, part)

    def send(stage, c, slot, src, dst, dst_sem, dom, blk):
        return pltpu.make_async_remote_copy(
            src_ref=src, dst_ref=dst, send_sem=send_sem.at[stage, c, slot], recv_sem=dst_sem,
            device_id=(dom, blk), device_id_type=MESH,
        )

    def arrived(stage, c, j, ref):
        pltpu.make_async_copy(ref.at[c, j], ref.at[c, j], recv_sem.at[stage, c, j]).wait()

    def own_arrow(c):
        return pltpu.make_async_copy(ain_hbm.at[rows_of(c)], prev_in.at[c, me], recv_sem.at[0, c, me])

    def arrow_copy(c, blk):
        return send(0, c, blk, ain_hbm.at[rows_of(c)], prev_in.at[c, me], recv_sem.at[0, c, me], t, blk)

    def mid_copy(c, blk):
        return send(1, c, blk, mid_mine.at[c], mid_in.at[c, me], recv_sem.at[1, c, me], t, blk)

    def row_copy(c, blk):
        return send(2, c, blk, row_mine.at[rows_of(c)], prev_in.at[c, me], recv_sem.at[0, c, me], after, blk)

    def cov_copy(c, blk):
        return send(3, c, blk, cov_part.at[c, blk], cov_in.at[c, me], recv_sem.at[2, c, me], t, blk)

    def on_copy(c, blk):
        return send(4, c, blk, on_part.at[c, blk], on_in.at[c, me], recv_sem.at[3, c, me], before, blk)

    def each(routes, body):
        for guard, blk in routes:
            pl.when(guard)(functools.partial(body, blk))

    def start(copy, c):
        return lambda blk: copy(c, blk).start()

    def left(copy, c):
        return lambda blk: copy(c, blk).wait_send()

    greeted = n - 1 + n * jnp.where(t > 0, 1, 0) + n * jnp.where(t < turns - 1, 1, 0)
    pl.semaphore_wait(barrier, greeted)

    @pl.when(t == 0)
    def _():
        for c in range(chunks):
            own_arrow(c).start()
            each(full, start(arrow_copy, c))

    loads[0].wait()
    for j in range(n):
        e_head[j], e_rest[j] = halves(e_raw[:, j * w:(j + 1) * w])
    loads[1].wait()
    loads[2].wait()
    for j in range(n):
        g_head[j], g_rest[j] = halves(g_raw[:, j * w:(j + 1) * w])
    loads[3].wait()
    loads[4].wait()

    for c in range(chunks):
        total = rhs[rows_of(c), :]
        for k in [0] + near:
            j = lax.rem(me + k, n)
            arrived(0, c, j, prev_in)
            total = total - product(stacked(prev_in[c, j]), e_head[j], e_rest[j], NT)
        mid_mine[c] = total
        each(up, start(mid_copy, c))

    for c in range(chunks):
        row_mine[rows_of(c), :] = product(stacked(mid_mine[c]), g_head[me], g_rest[me], NT)
        for k in range(1, n):
            @pl.when(me - k >= 0)
            def _(c=c, k=k):
                j = me - k
                arrived(1, c, j, mid_in)
                row_mine[rows_of(c), :] += product(stacked(mid_in[c, j]), g_head[j], g_rest[j], NT)

        @pl.when(t < turns - 1)
        def _(c=c):
            each(full, start(row_copy, c))
            row_copy(c, me).start()

    rows_out[0] = row_mine[...]
    tip_term = jnp.dot(tip[...], row_mine[...], precision=lax.Precision.HIGHEST)
    bnd[...] = jnp.where(t == turns - 1, bnd[...], 0.0) + tip_term

    for c in range(chunks):
        @pl.when(t < turns - 1)
        def _(c=c):
            for k in [0] + near:
                j = lax.rem(me + k, n)
                arrived(3, c, j, on_in)
                bnd[rows_of(c), :] += on_in[c, j]

        pair = stacked(-bnd[rows_of(c), :])
        def give_cov(j, c=c, pair=pair):
            cov_part[c, j] = product(pair, g_head[j], g_rest[j], NN)
            cov_copy(c, j).start()
        each(down, give_cov)
        cov_out[0, rows_of(c), :] = product(pair, g_head[me], g_rest[me], NN)

    for c in range(chunks):
        for k in range(1, n):
            @pl.when(me + k < n)
            def _(c=c, k=k):
                arrived(2, c, me + k, cov_in)
                cov_out[0, rows_of(c), :] += cov_in[c, me + k]

        @pl.when(t > 0)
        def _(c=c):
            pair = stacked(cov_out[0, rows_of(c), :])

            def give_on(j):
                on_part[c, j] = product(pair, e_head[j], e_rest[j], NN)
                on_copy(c, j).start()
            each(full, give_on)
            give_on(me)

    for c in range(chunks):
        @pl.when(t == 0)
        def _(c=c):
            each(full, left(arrow_copy, c))

        @pl.when(t < turns - 1)
        def _(c=c):
            each(full, left(row_copy, c))
            left(row_copy, c)(me)

        each(up, left(mid_copy, c))
        each(down, left(cov_copy, c))

        @pl.when(t > 0)
        def _(c=c):
            each(full, left(on_copy, c))
            left(on_copy, c)(me)


def solution(mesh):
    turns, n = mesh.shape["dom"], mesh.shape["blk"]

    def on_device(ginv, couple, arrow_rhs, arrow_in, tip_cov, bnd_next):
        a, w = arrow_in.shape
        whole = ginv.shape[2]
        chunks = CHUNKS
        part = a // chunks
        f32, bf16 = jnp.float32, jnp.bfloat16
        shape = jax.ShapeDtypeStruct((1, a, w), f32)
        blocks = pltpu.VMEM((chunks, n, part, w), f32)
        split = pltpu.VMEM((n, w, w), bf16)
        rows, cov = pl.pallas_call(
            functools.partial(kernel, turns, n, chunks),
            out_shape=(shape, shape),
            in_specs=[pl.BlockSpec(memory_space=pl.ANY)] * 6,
            out_specs=(pl.BlockSpec(memory_space=pltpu.VMEM),) * 2,
            scratch_shapes=[
                pltpu.VMEM((w, whole), f32),
                pltpu.VMEM((w, whole), f32),
                split, split, split, split,
                pltpu.VMEM((a, w), f32),
                pltpu.VMEM((a, a), f32),
                pltpu.VMEM((a, w), f32),
                blocks, blocks, blocks, blocks,
                pltpu.VMEM((chunks, part, w), f32),
                pltpu.VMEM((a, w), f32),
                blocks, blocks,
                pltpu.SemaphoreType.DMA((5,)),
                pltpu.SemaphoreType.DMA((5, chunks, n)),
                pltpu.SemaphoreType.DMA((4, chunks, n)),
            ],
            compiler_params=pltpu.CompilerParams(
                collective_id=0, has_side_effects=True, vmem_limit_bytes=48 * 1024 * 1024
            ),
        )(ginv, couple, arrow_rhs, arrow_in, tip_cov, bnd_next)
        return rows, cov

    return jax.shard_map(
        on_device,
        mesh=mesh,
        in_specs=(
            P("dom", "blk", None),
            P("dom", "blk", None),
            P("dom", None, "blk"),
            P(None, "blk"),
            P(),
            P(None, "blk"),
        ),
        out_specs=(P("dom", None, "blk"), P("dom", None, "blk")),
        check_vma=False,
    )
```

```python
import functools

import jax
import jax.numpy as jnp
from jax import lax
from jax.experimental import pallas as pl
from jax.experimental.pallas import tpu as pltpu
from jax.sharding import PartitionSpec as P

CHUNKS = 2


def ORDER(pairs):
    return range(1, pairs)


def PUT(routes, side):
    return [side] + routes

MESH = pl.DeviceIdType.MESH
NT = (((1,), (1,)), ((), ()))
NN = (((1,), (0,)), ((), ()))


def halves(x):
    head = x.astype(jnp.bfloat16)
    rest = (x - head.astype(jnp.float32)).astype(jnp.bfloat16)
    return head, rest


def stacked(x):
    head, rest = halves(x)
    return jnp.concatenate([head, rest], axis=0)


def product(pair, w_head, w_rest, dims):
    rows = pair.shape[0] // 2
    both = lax.dot_general(pair, w_head, dims, preferred_element_type=jnp.float32)
    cross = lax.dot_general(pair[:rows], w_rest, dims, preferred_element_type=jnp.float32)
    return both[:rows] + (both[rows:] + cross)


def around(n):
    order = []
    for k in range(1, n // 2 + 1):
        order += [k] if k == n - k else [k, n - k]
    return order


def kernel(
    turns, n, chunks,
    g_hbm, e_hbm, rhs_hbm, ain_hbm, tip_hbm, bnd_hbm,
    rows_out, cov_out,
    g_raw, e_raw, g_head, g_rest, e_head, e_rest, rhs, tip, bnd,
    prev_in, mid_in, cov_in, on_in, mid_mine, row_mine, cov_part, on_part,
    load_sem, send_sem, recv_sem,
):
    t = lax.axis_index("dom")
    me = lax.axis_index("blk")
    a, w = rhs.shape
    part = a // chunks
    near = around(n)
    pairs = n // 2
    p, y = lax.div(me, 2), lax.rem(me, 2)
    buddy = me + 1 - 2 * y
    before, after = t - 1, t + 1
    up, down, full = [], [], []
    for across in (1, 0):
        for d in ORDER(pairs):
            high = (p + d < pairs, 2 * (p + d) + (1 - y if across else y))
            low = (p - d >= 0, 2 * (p - d) + (1 - y if across else y))
            up.append(high)
            down.append(low)
            full += [high, low]
    side = (y >= 0, buddy)
    up, down, full = PUT(up, (y == 0, buddy)), PUT(down, (y == 1, buddy)), PUT(full, side)

    loads = [
        pltpu.make_async_copy(src, dst, load_sem.at[i])
        for i, (src, dst) in enumerate(
            [(e_hbm.at[0], e_raw), (rhs_hbm.at[0], rhs), (g_hbm.at[0], g_raw), (tip_hbm, tip), (bnd_hbm, bnd)]
        )
    ]
    for load in loads:
        load.start()

    barrier = pltpu.get_barrier_semaphore()

    def greet(dom, blk):
        pl.semaphore_signal(barrier, inc=1, device_id=(dom, blk), device_id_type=MESH)

    for k in near:
        greet(t, lax.rem(me + k, n))

    @pl.when(t > 0)
    def _():
        for k in range(n):
            greet(t - 1, lax.rem(me + k, n))

    @pl.when(t < turns - 1)
    def _():
        for k in range(n):
            greet(t + 1, lax.rem(me + k, n))

    def rows_of(c):
        return pl.ds(c * part, part)

    def send(stage, c, slot, src, dst, dst_sem, dom, blk):
        return pltpu.make_async_remote_copy(
            src_ref=src, dst_ref=dst, send_sem=send_sem.at[stage, c, slot], recv_sem=dst_sem,
            device_id=(dom, blk), device_id_type=MESH,
        )

    def arrived(stage, c, j, ref):
        pltpu.make_async_copy(ref.at[c, j], ref.at[c, j], recv_sem.at[stage, c, j]).wait()

    def own_arrow(c):
        return pltpu.make_async_copy(ain_hbm.at[rows_of(c)], prev_in.at[c, me], recv_sem.at[0, c, me])

    def arrow_copy(c, blk):
        return send(0, c, blk, ain_hbm.at[rows_of(c)], prev_in.at[c, me], recv_sem.at[0, c, me], t, blk)

    def mid_copy(c, blk):
        return send(1, c, blk, mid_mine.at[c], mid_in.at[c, me], recv_sem.at[1, c, me], t, blk)

    def row_copy(c, blk):
        return send(2, c, blk, row_mine.at[rows_of(c)], prev_in.at[c, me], recv_sem.at[0, c, me], after, blk)

    def cov_copy(c, blk):
        return send(3, c, blk, cov_part.at[c, blk], cov_in.at[c, me], recv_sem.at[2, c, me], t, blk)

    def on_copy(c, blk):
        return send(4, c, blk, on_part.at[c, blk], on_in.at[c, me], recv_sem.at[3, c, me], before, blk)

    def each(routes, body):
        for guard, blk in routes:
            pl.when(guard)(functools.partial(body, blk))

    def start(copy, c):
        return lambda blk: copy(c, blk).start()

    def left(copy, c):
        return lambda blk: copy(c, blk).wait_send()

    greeted = n - 1 + n * jnp.where(t > 0, 1, 0) + n * jnp.where(t < turns - 1, 1, 0)
    pl.semaphore_wait(barrier, greeted)

    @pl.when(t == 0)
    def _():
        for c in range(chunks):
            own_arrow(c).start()
            each(full, start(arrow_copy, c))

    loads[0].wait()
    for j in range(n):
        e_head[j], e_rest[j] = halves(e_raw[:, j * w:(j + 1) * w])
    loads[1].wait()
    loads[2].wait()
    for j in range(n):
        g_head[j], g_rest[j] = halves(g_raw[:, j * w:(j + 1) * w])
    loads[3].wait()
    loads[4].wait()

    for c in range(chunks):
        mid_mine[c] = rhs[rows_of(c), :]

        def take_prev(j, c=c):
            arrived(0, c, j, prev_in)
            mid_mine[c] -= product(stacked(prev_in[c, j]), e_head[j], e_rest[j], NT)
        take_prev(me)
        each(full, take_prev)
        each(up, start(mid_copy, c))

    for c in range(chunks):
        row_mine[rows_of(c), :] = product(stacked(mid_mine[c]), g_head[me], g_rest[me], NT)

        def take_mid(j, c=c):
            arrived(1, c, j, mid_in)
            row_mine[rows_of(c), :] += product(stacked(mid_in[c, j]), g_head[j], g_rest[j], NT)
        each(down, take_mid)

        @pl.when(t < turns - 1)
        def _(c=c):
            each(full, start(row_copy, c))
            row_copy(c, me).start()

    rows_out[0] = row_mine[...]
    tip_term = jnp.dot(tip[...], row_mine[...], precision=lax.Precision.HIGHEST)
    bnd[...] = jnp.where(t == turns - 1, bnd[...], 0.0) + tip_term

    for c in range(chunks):
        @pl.when(t < turns - 1)
        def _(c=c):
            for k in [0] + near:
                j = lax.rem(me + k, n)
                arrived(3, c, j, on_in)
                bnd[rows_of(c), :] += on_in[c, j]

        pair = stacked(-bnd[rows_of(c), :])
        def give_cov(j, c=c, pair=pair):
            cov_part[c, j] = product(pair, g_head[j], g_rest[j], NN)
            cov_copy(c, j).start()
        each(down, give_cov)
        cov_out[0, rows_of(c), :] = product(pair, g_head[me], g_rest[me], NN)

    for c in range(chunks):
        for k in range(1, n):
            @pl.when(me + k < n)
            def _(c=c, k=k):
                arrived(2, c, me + k, cov_in)
                cov_out[0, rows_of(c), :] += cov_in[c, me + k]

        @pl.when(t > 0)
        def _(c=c):
            pair = stacked(cov_out[0, rows_of(c), :])

            def give_on(j):
                on_part[c, j] = product(pair, e_head[j], e_rest[j], NN)
                on_copy(c, j).start()
            each(full, give_on)
            give_on(me)

    for c in range(chunks):
        @pl.when(t == 0)
        def _(c=c):
            each(full, left(arrow_copy, c))

        @pl.when(t < turns - 1)
        def _(c=c):
            each(full, left(row_copy, c))
            left(row_copy, c)(me)

        each(up, left(mid_copy, c))
        each(down, left(cov_copy, c))

        @pl.when(t > 0)
        def _(c=c):
            each(full, left(on_copy, c))
            left(on_copy, c)(me)


def solution(mesh):
    turns, n = mesh.shape["dom"], mesh.shape["blk"]

    def on_device(ginv, couple, arrow_rhs, arrow_in, tip_cov, bnd_next):
        a, w = arrow_in.shape
        whole = ginv.shape[2]
        chunks = CHUNKS
        part = a // chunks
        f32, bf16 = jnp.float32, jnp.bfloat16
        shape = jax.ShapeDtypeStruct((1, a, w), f32)
        blocks = pltpu.VMEM((chunks, n, part, w), f32)
        split = pltpu.VMEM((n, w, w), bf16)
        rows, cov = pl.pallas_call(
            functools.partial(kernel, turns, n, chunks),
            out_shape=(shape, shape),
            in_specs=[pl.BlockSpec(memory_space=pl.ANY)] * 6,
            out_specs=(pl.BlockSpec(memory_space=pltpu.VMEM),) * 2,
            scratch_shapes=[
                pltpu.VMEM((w, whole), f32),
                pltpu.VMEM((w, whole), f32),
                split, split, split, split,
                pltpu.VMEM((a, w), f32),
                pltpu.VMEM((a, a), f32),
                pltpu.VMEM((a, w), f32),
                blocks, blocks, blocks, blocks,
                pltpu.VMEM((chunks, part, w), f32),
                pltpu.VMEM((a, w), f32),
                blocks, blocks,
                pltpu.SemaphoreType.DMA((5,)),
                pltpu.SemaphoreType.DMA((5, chunks, n)),
                pltpu.SemaphoreType.DMA((4, chunks, n)),
            ],
            compiler_params=pltpu.CompilerParams(
                collective_id=0, has_side_effects=True
            ),
        )(ginv, couple, arrow_rhs, arrow_in, tip_cov, bnd_next)
        return rows, cov

    return jax.shard_map(
        on_device,
        mesh=mesh,
        in_specs=(
            P("dom", "blk", None),
            P("dom", "blk", None),
            P("dom", None, "blk"),
            P(None, "blk"),
            P(),
            P(None, "blk"),
        ),
        out_specs=(P("dom", None, "blk"), P("dom", None, "blk")),
        check_vma=False,
    )
```
